512 devices in a mesh: row: 16 (over x, y_hi), col: 32 (over z, y_lo, core).
Axes of the slice: x: 4, y: 8 (y_hi: 4, y_lo: 2; y = y_hi * 2 + y_lo), z: 8, core: 2. Of those that a mesh axis runs over, the one named last changes fastest.
Arguments:
- adjoint: bfloat16 [64, 65536], P(None, ('row', 'col')), may hold values from -6 to 6
- panel_order: int32 [16, 4096], P('row'), may hold values from 0 to 4095, each once within a row
- left_factor: bfloat16 [256, 256, 16, 256], P('row', 'col'), may hold values from -0.375 to 0.375
- right_factor: bfloat16 [256, 256, 16, 256], P('row', 'col'), may hold values from -0.09375 to 0.09375
- tile_ranks: int32 [256, 256], P('row', 'col'), may hold values from 1 to 16
- near_blocks: bfloat16 [16, 32, 8, 256, 256], P('row', 'col'), may hold values from -0.1875 to 0.1875
- near_index: int32 [16, 32, 2, 8], P('row', 'col'), may hold values from 0 to 15, as said below
- near_count: int32 [16, 32], P('row', 'col'), may hold values from 1 to 8, as said below
Outputs:
- result: float32 [64, 65536], P(None, ('col', 'row'))
The draws below stay inside these ranges and needn't reach their ends.
Inputs may be any that keep to these rules, and one draw needn't show every extreme that they name: `near_index`: the 8 slots of one device name distinct tiles of its 16 x 8 block. `near_count`: some device uses all 8 slots.
All inputs are finite; a program needn't handle non-finite values.
Results may differ from the reference program's by a relative error of at most 0.0017.
Values may be sent and summed in bfloat16 or wider, within the bound.
A program may use at most 64 MiB of HBM per device.

```python
import jax
import jax.numpy as jnp
from jax import lax

K = 64
B = 256
RMAX = 16
RT = 16
CT = 8
NEAR_CAP = 8
TR = 256
TC = 256
NR = 65536
N_ROW = 16
N_COL = 32


def draw_near_index(key, part):
    keys = jax.random.split(jax.random.fold_in(key, 11), N_ROW * N_COL)

    def one_device(device_key):
        chosen = jax.random.permutation(device_key, RT * CT)[:NEAR_CAP].astype(jnp.int32)
        return jnp.stack([chosen // CT, chosen % CT], axis=0)
    return jax.vmap(one_device)(keys).reshape(N_ROW, N_COL, 2, NEAR_CAP).astype(jnp.int32)


def draw_near_count(key, part):
    first_key, second_key, third_key = jax.random.split(jax.random.fold_in(key, 23), 3)
    first = jax.random.randint(first_key, (N_ROW * N_COL,), 0, NEAR_CAP)
    second = jax.random.randint(second_key, (N_ROW * N_COL,), 0, NEAR_CAP)
    counts = 1 + first * second // NEAR_CAP
    chosen = jax.random.randint(third_key, (), 0, N_ROW * N_COL)
    counts = jnp.where(jnp.arange(N_ROW * N_COL) == chosen, NEAR_CAP, counts)
    return counts.reshape(N_ROW, N_COL).astype(jnp.int32)


def with_ends(entries, rng, least, largest):
    extent = entries.shape
    index_at = [jax.random.randint(jax.random.fold_in(rng, axis), (), 0, extent[axis]) for axis in range(len(extent))]
    entries = entries.at[tuple(index_at)].set(least)
    longest = extent.index(max(extent))
    index_at[longest] = (index_at[longest] + 1) % extent[longest]
    return entries.at[tuple(index_at)].set(largest)


def level_of(key, dims, cuts, low, top_value):
    def one(position, shards_of):
        heights = jax.random.uniform(jax.random.fold_in(jax.random.fold_in(key, 6), position), (shards_of,), jnp.float32, low / len(cuts), top_value / len(cuts))
        return jnp.repeat(jnp.exp(heights), dims[position] // shards_of).reshape((-1,) + (1,) * (len(dims) - position - 1))

    level = one(*cuts[0])
    for cut in cuts[1:]:
        level = level * one(*cut)
    return level


def normal_values(rng, extent, spread, most, cuts=(), held_as=jnp.bfloat16):
    entries = jax.random.normal(rng, extent, jnp.float32) * spread
    if len(cuts) > 0:
        entries = level_of(rng, extent, cuts, -0.22, 0.18) * entries
    return jnp.clip(entries, min=-most, max=most).astype(held_as)


def setup_inputs(seed: int = 0) -> dict:
    arg_keys = jax.random.split(jax.random.key(seed), 9)
    adjoint = normal_values(arg_keys[0], (K, NR), 1.0, 6.0, ((1, 512),))
    panel_order = jax.vmap(lambda own: jax.random.permutation(own, RT * B))(jax.random.split(arg_keys[1], N_ROW)).reshape((N_ROW, RT * B)).astype(jnp.int32)
    left_factor = normal_values(arg_keys[2], (TR, TC, RMAX, B), B ** -0.5, 0.375, ((0, 16), (1, 32)))
    right_factor = normal_values(arg_keys[3], (TR, TC, RMAX, B), (TR * RMAX) ** -0.5, 0.09375, ((0, 16), (1, 32)))
    tile_ranks = with_ends(jax.random.randint(arg_keys[4], (TR, TC), 1, RMAX + 1), jax.random.fold_in(arg_keys[4], 1), 1, RMAX).astype(jnp.int32)
    near_blocks = normal_values(arg_keys[5], (N_ROW, N_COL, NEAR_CAP, B, B), (4 * B) ** -0.5, 0.1875, ((0, 16), (1, 32)))
    near_index = draw_near_index(jax.random.fold_in(arg_keys[8], 71), 0)
    near_count = draw_near_count(jax.random.fold_in(arg_keys[8], 71), 0)
    return {"adjoint": adjoint, "panel_order": panel_order, "left_factor": left_factor, "right_factor": right_factor, "tile_ranks": tile_ranks, "near_blocks": near_blocks, "near_index": near_index, "near_count": near_count}


def reference(adjoint, panel_order, left_factor, right_factor, tile_ranks, near_blocks, near_index, near_count):
    group_cols = RT * B
    grouped = adjoint.reshape(K, N_ROW, group_cols)
    rank_range = jnp.arange(RMAX, dtype=jnp.int32)
    slot_range = jnp.arange(NEAR_CAP, dtype=jnp.int32)
    tile_range = jnp.arange(CT, dtype=jnp.int32)

    def one_group(carry, group):
        source = lax.dynamic_index_in_dim(grouped, group, 1, keepdims=False)
        order_row = lax.dynamic_index_in_dim(panel_order, group, 0, keepdims=False)
        tiled = jnp.take(source, order_row, axis=1).reshape(K, RT, B)
        left_part = lax.dynamic_slice_in_dim(left_factor, group * RT, RT, 0)
        right_part = lax.dynamic_slice_in_dim(right_factor, group * RT, RT, 0)
        rank_part = lax.dynamic_slice_in_dim(tile_ranks, group * RT, RT, 0)
        projected = jnp.einsum("kab,acrb->ackr", tiled.astype(jnp.float32), left_part.astype(jnp.float32), precision=lax.Precision.HIGHEST)
        keep = (rank_range[None, None, :] < rank_part[:, :, None])[:, :, None, :]
        projected = jnp.where(keep, projected, 0.0).astype(jnp.bfloat16)
        far_part = jnp.einsum("ackr,acrb->kcb", projected.astype(jnp.float32), right_part.astype(jnp.float32), precision=lax.Precision.HIGHEST)
        blocks = lax.dynamic_index_in_dim(near_blocks, group, 0, keepdims=False)
        index_part = lax.dynamic_index_in_dim(near_index, group, 0, keepdims=False)
        count_part = lax.dynamic_index_in_dim(near_count, group, 0, keepdims=False)
        picked = tiled[:, index_part[:, 0, :], :]
        product = jnp.einsum("kjnb,jnbc->kjnc", picked.astype(jnp.float32), blocks.astype(jnp.float32), precision=lax.Precision.HIGHEST)
        valid = slot_range[None, :] < count_part[:, None]
        product = jnp.where(valid[None, :, :, None], product, 0.0)
        onehot = (index_part[:, 1, :, None] == tile_range[None, None, :]).astype(jnp.float32)
        near_part = jnp.einsum("kjnc,jnt->kjtc", product, onehot, precision=lax.Precision.HIGHEST).reshape(K, N_COL * CT, B)
        return carry + far_part + near_part, None

    total, _ = lax.scan(one_group, jnp.zeros((K, N_COL * CT, B), jnp.float32), jnp.arange(N_ROW, dtype=jnp.int32))
    return total.reshape(K, N_COL * CT * B)
```

```python
import functools

import jax
import jax.numpy as jnp
from jax import lax
from jax.experimental import pallas as pl
from jax.experimental.pallas import tpu as pltpu
from jax.sharding import PartitionSpec as P

MESH = pl.DeviceIdType.MESH
F32 = jnp.float32
BF16 = jnp.bfloat16

NZ = 8
NX = 4
NY = 4
K = 64
B = 256
W = 128
RT = 16
CT = 8
R = 16
SLOTS = 8


def kernel(
    index_ref, count_ref, rank_ref, order_ref, a_hbm, left_hbm, right_hbm, near_hbm, out_ref,
    left, right, near, hot, high, held, xs, proj, sbuf, xbuf, acc, ybuf,
    load_sem, zsend, zrecv, ysend, yrecv, csend, crecv, xsend, xrecv, vsend, vrecv,
):
    g = lax.axis_index("row")
    h = lax.axis_index("col")
    z, part = h // 4, h % 4
    ypart = (part + 2) % 4
    cpart = part + 1 - 2 * (part % 2)
    x, v = g // NY, g % NY
    ypeer = z * 4 + ypart
    cpeer = z * 4 + cpart

    barrier = pltpu.get_barrier_semaphore()
    zpeers = [((z + d) % NZ) * 4 + part for d in range(1, NZ)]
    xpeers = [((x + d) % NX) * NY + v for d in range(1, NX)]
    vpeers = [x * NY + (v + d) % NY for d in range(1, NY)]
    for peer in zpeers + [ypeer, cpeer]:
        pl.semaphore_signal(barrier, inc=1, device_id={"col": peer}, device_id_type=MESH)
    for peer in xpeers + vpeers:
        pl.semaphore_signal(barrier, inc=1, device_id={"row": peer}, device_id_type=MESH)

    def block_of(which, dz):
        source = (z + NZ - dz) % NZ
        return held.at[which, :, pl.ds(pl.multiple_of(source * W, W), W)]

    own = pltpu.make_async_copy(a_hbm, block_of(part, 0), load_sem.at[0])
    own.start()
    loads = [
        pltpu.make_async_copy(src, dst, load_sem.at[1 + i])
        for i, (src, dst) in enumerate(((left_hbm, left), (right_hbm, right), (near_hbm, near)))
    ]
    for load in loads:
        load.start()

    pl.semaphore_wait(barrier, len(zpeers) + 2 + len(xpeers) + len(vpeers))

    copies = []

    def send(src, dst, ssem, rsem, axis, peer):
        copy = pltpu.make_async_remote_copy(
            src_ref=src, dst_ref=dst, send_sem=ssem, recv_sem=rsem,
            device_id={axis: peer}, device_id_type=MESH,
        )
        copy.start()
        copies.append(copy)
        return copy

    zcopies = {}
    for d in (4, 3, 5, 2, 6, 1, 7):
        zcopies[d] = send(
            a_hbm, block_of(part, 0), zsend.at[d - 1], zrecv.at[d - 1], "col", zpeers[d - 1]
        )
    ycopies = {0: send(a_hbm, block_of(part, 0), ysend.at[0], yrecv.at[0], "col", ypeer)}
    ccopies = {0: send(a_hbm, block_of(part, 0), csend.at[0], crecv.at[0], "col", cpeer)}

    def build(t, carry):
        source = order_ref[t]
        low = (source // 512) * W + source % W
        high[t] = (source // W) % 4
        low = jnp.broadcast_to(low, (R, B))
        row = lax.broadcasted_iota(jnp.int32, (R, B), 0)
        for i in range(NZ * W // R):
            hot[t, i * R : (i + 1) * R, :] = jnp.where(low == row + i * R, 1.0, 0.0).astype(BF16)
        return carry

    lax.fori_loop(0, RT, build, 0)

    for d in (1, 7, 2, 6, 3, 5, 4):
        zcopies[d].wait_recv()
        block = block_of(part, d)
        ycopies[d] = send(block, block, ysend.at[d], yrecv.at[d], "col", ypeer)
        ccopies[d] = send(block, block, csend.at[d], crecv.at[d], "col", cpeer)
    for d in (0, 1, 7, 2, 6, 3, 5, 4):
        ycopies[d].wait_recv()
        block = block_of(ypart, d)
        ccopies[8 + d] = send(block, block, csend.at[8 + d], crecv.at[8 + d], "col", cpeer)
    own.wait()
    for load in loads:
        load.wait()
    for d in range(16):
        ccopies[d].wait_recv()

    rank_row = lax.broadcasted_iota(jnp.int32, (R, K), 0)

    def tile(t, carry):
        spread = jnp.dot(
            held[...].reshape(4 * K, NZ * W), hot[t], preferred_element_type=F32
        )
        which = jnp.broadcast_to(high[t], (K, B))
        picked = spread[0:K]
        for i in range(1, 4):
            picked = jnp.where(which == i, spread[i * K : (i + 1) * K], picked)
        picked = picked.astype(BF16)
        xs[t] = picked
        value = lax.dot_general(
            left[t].reshape(CT * R, B), picked, (((1,), (1,)), ((), ())),
            preferred_element_type=F32,
        )
        for c in range(CT):
            keep = rank_row < rank_ref[t, c]
            proj[t, c] = jnp.where(keep, value[c * R : (c + 1) * R], 0.0).astype(BF16)
        return carry

    lax.fori_loop(0, RT, tile, 0)

    products = []
    for n in range(SLOTS):
        lhs = xs[index_ref[0, 0, 0, n]]
        products.append(jnp.dot(lhs, near[n], preferred_element_type=F32))

    def column_tile(c):
        total = lax.dot_general(
            proj[:, c].reshape(RT * R, K), right[:, c].reshape(RT * R, B),
            (((0,), (0,)), ((), ())), preferred_element_type=F32,
        )
        for n in range(SLOTS):
            used = jnp.logical_and(index_ref[0, 0, 1, n] == c, n < count_ref[0, 0])
            total = total + jnp.where(used, products[n], 0.0)
        return total

    xcopies = {}
    for d in (2, 1, 3, 0):
        to = (x + d) % NX
        for j in range(2):
            total = column_tile(to * 2 + j)
            if d == 0:
                acc[2 * j] = total[:, :W]
                acc[2 * j + 1] = total[:, W:]
            else:
                sbuf[d - 1, :, j * B : (j + 1) * B] = total.astype(BF16)
        if d > 0:
            xcopies[d] = send(
                sbuf.at[d - 1], xbuf.at[d - 1], xsend.at[d - 1], xrecv.at[d - 1],
                "row", xpeers[d - 1],
            )
    for d in (1, 3, 2):
        xcopies[d].wait_recv()
    for j in range(NY):
        total = acc[j]
        for d in range(1, NX):
            total = total + xbuf[d - 1, :, j * W : (j + 1) * W].astype(F32)
        acc[j] = total
    vcopies = {}
    for e in (2, 1, 3):
        vcopies[e] = send(
            acc.at[(v + e) % NY], ybuf.at[e - 1], vsend.at[e - 1], vrecv.at[e - 1],
            "row", vpeers[e - 1],
        )
    total = acc[v]
    for e in (1, 3, 2):
        vcopies[e].wait_recv()
        total = total + ybuf[e - 1]
    out_ref[...] = total
    for copy in copies:
        copy.wait_send()


def local(
    adjoint, panel_order, left_factor, right_factor, tile_ranks, near_blocks, near_index, near_count
):
    smem = pl.BlockSpec(memory_space=pltpu.SMEM)
    vmem = pl.BlockSpec(memory_space=pltpu.VMEM)
    hbm = pl.BlockSpec(memory_space=pltpu.HBM)
    dma = pltpu.SemaphoreType.DMA
    return pl.pallas_call(
        kernel,
        out_shape=jax.ShapeDtypeStruct((K, W), F32),
        in_specs=[smem, smem, smem, vmem, hbm, hbm, hbm, hbm],
        out_specs=vmem,
        scratch_shapes=[
            pltpu.VMEM((RT, CT, R, B), BF16),
            pltpu.VMEM((RT, CT, R, B), BF16),
            pltpu.VMEM((SLOTS, B, B), BF16),
            pltpu.VMEM((RT, NZ * W, B), BF16),
            pltpu.VMEM((RT, 1, B), jnp.int32),
            pltpu.VMEM((4, K, NZ * W), BF16),
            pltpu.VMEM((RT, K, B), BF16),
            pltpu.VMEM((RT, CT, R, K), BF16),
            pltpu.VMEM((NX - 1, K, NY * W), BF16),
            pltpu.VMEM((NX - 1, K, NY * W), BF16),
            pltpu.VMEM((NY, K, W), F32),
            pltpu.VMEM((NY - 1, K, W), F32),
            dma((4,)), dma((7,)), dma((7,)), dma((8,)), dma((8,)), dma((16,)), dma((16,)),
            dma((3,)), dma((3,)), dma((3,)), dma((3,)),
        ],
        compiler_params=pltpu.CompilerParams(
            collective_id=0, has_side_effects=True, vmem_limit_bytes=60 << 20
        ),
    )(
        near_index, near_count, tile_ranks, panel_order.reshape(RT, 1, B), adjoint,
        left_factor, right_factor, near_blocks[0, 0],
    )


def solution(mesh):
    placed = (
        P(None, ("row", "col")),
        P("row", None),
        P("row", "col", None, None),
        P("row", "col", None, None),
        P("row", "col"),
        P("row", "col", None, None, None),
        P("row", "col", None, None),
        P("row", "col"),
    )
    return jax.shard_map(
        local, mesh=mesh, in_specs=placed, out_specs=P(None, ("col", "row")), check_vma=False
    )
```

```python
import jax
import jax.numpy as jnp
from jax import lax
from jax.experimental import pallas as pl
from jax.experimental.pallas import tpu as pltpu
from jax.sharding import PartitionSpec as P

MESH = pl.DeviceIdType.MESH
F32 = jnp.float32
BF16 = jnp.bfloat16

NZ = 8
NX = 4
NY = 4
K = 64
B = 256
W = 128
RT = 16
CT = 8
R = 16
SLOTS = 8

ARRIVAL = (0, 1, 7, 2, 6, 3, 5, 4)
SLOT = {d: s for s, d in enumerate(ARRIVAL)}
DIRECT = (3, 5, 4)
CHUNKS = ((0, 4), (4, 6), (6, 8))


def kernel(
    index_ref, count_ref, rank_ref, order_ref, a_hbm, left_hbm, right_hbm, near_hbm, out_ref,
    own, left, right, near, hot, high, held, spread, xs, proj, sbuf, xbuf, acc, vbuf, ybuf,
    load_sem, zsend, zrecv, ysend, yrecv, csend, crecv, dsend, drecv, xsend, xrecv, vsend, vrecv,
):
    g = lax.axis_index("row")
    h = lax.axis_index("col")
    z, part = h // 4, h % 4
    x, v = g // NY, g % NY
    cpeer = z * 4 + part + 1 - 2 * (part % 2)
    ypeer = z * 4 + (part + 2) % 4
    dpeer = z * 4 + 3 - part
    zpeers = [((z + d) % NZ) * 4 + part for d in range(1, NZ)]
    xpeers = [((x + d) % NX) * NY + v for d in range(1, NX)]
    vpeers = [x * NY + (v + d) % NY for d in range(1, NY)]

    barrier = pltpu.get_barrier_semaphore()
    for peer in zpeers + [ypeer, cpeer, dpeer]:
        pl.semaphore_signal(barrier, inc=1, device_id={"col": peer}, device_id_type=MESH)
    for peer in xpeers + vpeers:
        pl.semaphore_signal(barrier, inc=1, device_id={"row": peer}, device_id_type=MESH)

    mine = pltpu.make_async_copy(a_hbm, own, load_sem.at[0])
    mine.start()
    loads = [
        pltpu.make_async_copy(src, dst, load_sem.at[1 + i])
        for i, (src, dst) in enumerate(((left_hbm, left), (right_hbm, right), (near_hbm, near)))
    ]
    for load in loads:
        load.start()
    mine.wait()
    pl.semaphore_wait(barrier, len(zpeers) + 3 + len(xpeers) + len(vpeers))

    copies = []

    def send(src, dst, ssem, rsem, axis, peer):
        copy = pltpu.make_async_remote_copy(
            src_ref=src, dst_ref=dst, send_sem=ssem, recv_sem=rsem,
            device_id={axis: peer}, device_id_type=MESH,
        )
        copy.start()
        copies.append(copy)
        return copy

    zcopy, ycopy, ccopy, dcopy = {}, {}, {}, {}
    for d in (4, 3, 5, 2, 6, 1, 7):
        zcopy[d] = send(
            own, held.at[SLOT[d], 0], zsend.at[d - 1], zrecv.at[d - 1], "col", zpeers[d - 1]
        )

    def forward(d):
        block = held.at[SLOT[d], 0] if d else own
        s = SLOT[d]
        ycopy[d] = send(block, held.at[s, 2], ysend.at[s], yrecv.at[s], "col", ypeer)
        if d in DIRECT:
            dcopy[d] = send(block, held.at[s, 3], dsend.at[s], drecv.at[s], "col", dpeer)
        ccopy[d] = send(block, held.at[s, 1], csend.at[s], crecv.at[s], "col", cpeer)

    def relay(d):
        s = SLOT[d]
        ycopy[d].wait_recv()
        if d not in DIRECT:
            block = held.at[s, 2]
            dcopy[d] = send(block, held.at[s, 3], dsend.at[s], drecv.at[s], "col", cpeer)

    forward(0)
    held[0, 0] = own[...]

    def build(t, carry):
        source = order_ref[t]
        device = source // W
        dz = lax.rem(z + NZ - device // 4, NZ)
        slot = jnp.where(dz <= 4, jnp.maximum(2 * dz - 1, 0), 16 - 2 * dz)
        high[t] = lax.rem(device, 4) ^ part
        low = jnp.broadcast_to(slot * W + lax.rem(source, W), (R, B)).astype(jnp.int16)
        row = lax.broadcasted_iota(jnp.int32, (R, B), 0).astype(jnp.int16)
        one, zero = jnp.ones((R, B), BF16), jnp.zeros((R, B), BF16)
        for i in range(NZ * W // R):
            hot[t, i * R : (i + 1) * R, :] = jnp.where(low == row + jnp.int16(i * R), one, zero)
        return carry

    lax.fori_loop(0, RT, build, 0)

    for d in ARRIVAL[1:]:
        zcopy[d].wait_recv()
        forward(d)
    for d in ARRIVAL:
        if d not in DIRECT:
            relay(d)

    for first, last in CHUNKS:
        for d in ARRIVAL[first:last]:
            if d in DIRECT:
                relay(d)
            ccopy[d].wait_recv()
            dcopy[d].wait_recv()
        lhs = jnp.concatenate(
            [held[s].reshape(4 * K, W) for s in range(first, last)], axis=1
        )
        for t in range(RT):
            share = jnp.dot(lhs, hot[t, first * W : last * W, :], preferred_element_type=F32)
            if first > 0:
                share = share + spread[t]
            if last < NZ:
                spread[t] = share
            else:
                which = jnp.broadcast_to(high[t], (K, B))
                picked = share[:K]
                for i in range(1, 4):
                    picked = jnp.where(which == i, share[i * K : (i + 1) * K], picked)
                xs[t] = picked.astype(BF16)

    for load in loads:
        load.wait()
    rank_row = lax.broadcasted_iota(jnp.int32, (R, K), 0)
    for t in range(RT):
        value = lax.dot_general(
            left[t].reshape(CT * R, B), xs[t], (((1,), (1,)), ((), ())),
            preferred_element_type=F32,
        )
        for c in range(CT):
            keep = rank_row < rank_ref[c, t]
            proj[t, c] = jnp.where(keep, value[c * R : (c + 1) * R], 0.0).astype(BF16)

    products = []
    for n in range(SLOTS):
        lhs = xs[index_ref[0, n]]
        products.append(jnp.dot(lhs, near[n], preferred_element_type=F32))

    def column_tile(c):
        total = lax.dot_general(
            proj[:, c].reshape(RT * R, K), right[:, c].reshape(RT * R, B),
            (((0,), (0,)), ((), ())), preferred_element_type=F32,
        )
        for n in range(SLOTS):
            used = jnp.logical_and(index_ref[1, n] == c, n < count_ref[0, 0])
            total = total + jnp.where(used, products[n], 0.0)
        return total

    for d in (2, 1, 3, 0):
        to = (x + d) % NX
        for j in range(2):
            total = column_tile(to * 2 + j)
            for i in range(2):
                half = total[:, i * W : (i + 1) * W]
                if d == 0:
                    acc[2 * j + i] = half
                else:
                    sbuf[d - 1, 2 * j + i] = half.astype(BF16)

    xcopy, vcopy = {}, {}
    for e in (2, 1, 3, 0):
        for d in (2, 1, 3):
            xcopy[d, e] = send(
                sbuf.at[d - 1, (v + e) % NY], xbuf.at[d - 1, e],
                xsend.at[d - 1, e], xrecv.at[d - 1, e], "row", xpeers[d - 1],
            )

    def row_sum(e):
        total = acc[(v + e) % NY]
        for d in (1, 3, 2):
            xcopy[d, e].wait_recv()
        for d in (1, 3, 2):
            total = total + xbuf[d - 1, e].astype(F32)
        return total

    for e in (2, 1, 3):
        vbuf[e - 1] = row_sum(e)
        vcopy[e] = send(
            vbuf.at[e - 1], ybuf.at[e - 1], vsend.at[e - 1], vrecv.at[e - 1],
            "row", vpeers[e - 1],
        )
    total = row_sum(0)
    for e in (1, 3, 2):
        vcopy[e].wait_recv()
        total = total + ybuf[e - 1]
    out_ref[...] = total
    for copy in copies:
        copy.wait_send()


def local(
    adjoint, panel_order, left_factor, right_factor, tile_ranks, near_blocks, near_index, near_count
):
    smem = pl.BlockSpec(memory_space=pltpu.SMEM)
    vmem = pl.BlockSpec(memory_space=pltpu.VMEM)
    hbm = pl.BlockSpec(memory_space=pl.ANY)
    dma = pltpu.SemaphoreType.DMA
    return pl.pallas_call(
        kernel,
        out_shape=jax.ShapeDtypeStruct((K, W), F32),
        in_specs=[smem, smem, smem, vmem, hbm, hbm, hbm, hbm],
        out_specs=vmem,
        scratch_shapes=[
            pltpu.VMEM((K, W), BF16),
            pltpu.VMEM((RT, CT, R, B), BF16),
            pltpu.VMEM((RT, CT, R, B), BF16),
            pltpu.VMEM((SLOTS, B, B), BF16),
            pltpu.VMEM((RT, NZ * W, B), BF16),
            pltpu.VMEM((RT, 1, B), jnp.int32),
            pltpu.VMEM((NZ, 4, K, W), BF16),
            pltpu.VMEM((RT, 4 * K, B), F32),
            pltpu.VMEM((RT, K, B), BF16),
            pltpu.VMEM((RT, CT, R, K), BF16),
            pltpu.VMEM((NX - 1, NY, K, W), BF16),
            pltpu.VMEM((NX - 1, NY, K, W), BF16),
            pltpu.VMEM((NY, K, W), F32),
            pltpu.VMEM((NY - 1, K, W), F32),
            pltpu.VMEM((NY - 1, K, W), F32),
            dma((4,)), dma((7,)), dma((7,)), dma((8,)), dma((8,)), dma((8,)), dma((8,)),
            dma((8,)), dma((8,)), dma((3, 4)), dma((3, 4)), dma((3,)), dma((3,)),
        ],
        compiler_params=pltpu.CompilerParams(
            collective_id=0, has_side_effects=True, vmem_limit_bytes=60 << 20
        ),
    )(
        near_index[0, 0], near_count, tile_ranks.T, panel_order.reshape(RT, 1, B), adjoint,
        left_factor, right_factor, near_blocks[0, 0],
    )


def solution(mesh):
    placed = (
        P(None, ("row", "col")),
        P("row", None),
        P("row", "col", None, None),
        P("row", "col", None, None),
        P("row", "col"),
        P("row", "col", None, None, None),
        P("row", "col", None, None),
        P("row", "col"),
    )
    return jax.shard_map(
        local, mesh=mesh, in_specs=placed, out_specs=P(None, ("col", "row")), check_vma=False
    )
```

```python
import jax
import jax.numpy as jnp
from jax import lax
from jax.experimental import pallas as pl
from jax.experimental.pallas import tpu as pltpu
from jax.sharding import PartitionSpec as P

MESH = pl.DeviceIdType.MESH
F32 = jnp.float32
BF16 = jnp.bfloat16

NZ = 8
NX = 4
NY = 4
K = 64
B = 256
W = 128
RT = 16
CT = 8
R = 16
SLOTS = 8

ARRIVAL = (0, 1, 7, 2, 6, 3, 5, 4)
SLOT = {d: s for s, d in enumerate(ARRIVAL)}
DIRECT = (3, 5, 4)
CHUNKS = ((0, 4), (4, 6), (6, 8))


def encode(value, ref):
    groups = value.reshape(8, 8, W)
    most = jnp.maximum(jnp.max(jnp.abs(groups), axis=0), 1e-30)
    power = jnp.floor(jnp.log2(most))
    coded = jnp.round(groups * jnp.exp2(13.0 - power)[None]).reshape(K, W)
    ref[:K] = coded.astype(jnp.int32).astype(jnp.int16)
    power = power.astype(jnp.int32)
    ref[K:] = jnp.concatenate([power, power], axis=0).astype(jnp.int16)


def decode(ref):
    power = ref[K:].astype(jnp.int32)[:8].astype(F32)
    groups = ref[:K].astype(jnp.int32).astype(F32).reshape(8, 8, W)
    return (groups * jnp.exp2(power - 13.0)[None]).reshape(K, W)


def kernel(
    index_hbm, count_ref, rank_hbm, order_hbm, a_hbm, left_hbm, right_hbm, near_hbm, out_ref,
    index_ref, rank_ref, order_ref, own, left, right, near, hot, high, held, spread, xs, proj,
    sbuf, xbuf, acc, vbuf, ybuf,
    load_sem, zsend, zrecv, ysend, yrecv, csend, crecv, dsend, drecv, xsend, xrecv, vsend, vrecv,
):
    g = lax.axis_index("row")
    h = lax.axis_index("col")
    z, part = h // 4, h % 4
    x, v = g // NY, g % NY
    cpeer = z * 4 + part + 1 - 2 * (part % 2)
    ypeer = z * 4 + (part + 2) % 4
    dpeer = z * 4 + 3 - part
    zpeers = [((z + d) % NZ) * 4 + part for d in range(1, NZ)]
    xpeers = [((x + d) % NX) * NY + v for d in range(1, NX)]
    vpeers = [x * NY + (v + d) % NY for d in range(1, NY)]

    mine, ordering, *loads = [
        pltpu.make_async_copy(src, dst, load_sem.at[i])
        for i, (src, dst) in enumerate((
            (a_hbm, own), (order_hbm, order_ref), (left_hbm, left), (right_hbm, right),
            (near_hbm, near), (rank_hbm, rank_ref), (index_hbm, index_ref),
        ))
    ]
    mine.start()
    ordering.start()

    barrier = pltpu.get_barrier_semaphore()
    for peer in zpeers + [ypeer, cpeer, dpeer]:
        pl.semaphore_signal(barrier, inc=1, device_id={"col": peer}, device_id_type=MESH)
    for peer in xpeers + vpeers:
        pl.semaphore_signal(barrier, inc=1, device_id={"row": peer}, device_id_type=MESH)

    pl.semaphore_wait(barrier, len(zpeers) + 3 + len(xpeers) + len(vpeers))
    mine.wait()

    copies = []

    def send(src, dst, ssem, rsem, axis, peer):
        copy = pltpu.make_async_remote_copy(
            src_ref=src, dst_ref=dst, send_sem=ssem, recv_sem=rsem,
            device_id={axis: peer}, device_id_type=MESH,
        )
        copy.start()
        copies.append(copy)
        return copy

    zcopy, ycopy, ccopy, dcopy = {}, {}, {}, {}
    for d in (4, 3, 5, 2, 6, 1, 7):
        zcopy[d] = send(
            own, held.at[SLOT[d], 0], zsend.at[d - 1], zrecv.at[d - 1], "col", zpeers[d - 1]
        )

    def forward(d):
        block = held.at[SLOT[d], 0] if d else own
        s = SLOT[d]
        ycopy[d] = send(block, held.at[s, 2], ysend.at[s], yrecv.at[s], "col", ypeer)
        if d in DIRECT:
            dcopy[d] = send(block, held.at[s, 3], dsend.at[s], drecv.at[s], "col", dpeer)
        ccopy[d] = send(block, held.at[s, 1], csend.at[s], crecv.at[s], "col", cpeer)

    def relay(d):
        s = SLOT[d]
        ycopy[d].wait_recv()
        if d not in DIRECT:
            block = held.at[s, 2]
            dcopy[d] = send(block, held.at[s, 3], dsend.at[s], drecv.at[s], "col", cpeer)

    forward(0)
    for load in loads:
        load.start()
    held[0, 0] = own[...]

    ordering.wait()

    def build(t, carry):
        source = order_ref[t]
        device = source // W
        dz = lax.rem(z + NZ - device // 4, NZ)
        slot = jnp.where(dz <= 4, jnp.maximum(2 * dz - 1, 0), 16 - 2 * dz)
        high[t] = lax.rem(device, 4) ^ part
        low = jnp.broadcast_to(slot * W + lax.rem(source, W), (R, B)).astype(jnp.int16)
        row = lax.broadcasted_iota(jnp.int32, (R, B), 0).astype(jnp.int16)
        one, zero = jnp.ones((R, B), BF16), jnp.zeros((R, B), BF16)
        for i in range(NZ * W // R):
            hot[t, i * R : (i + 1) * R, :] = jnp.where(low == row + jnp.int16(i * R), one, zero)
        return carry

    lax.fori_loop(0, RT, build, 0)

    for d in ARRIVAL[1:]:
        zcopy[d].wait_recv()
        forward(d)
    for d in ARRIVAL:
        if d not in DIRECT:
            relay(d)

    for first, last in CHUNKS:
        for d in ARRIVAL[first:last]:
            if d in DIRECT:
                relay(d)
            ccopy[d].wait_recv()
            dcopy[d].wait_recv()
        lhs = jnp.concatenate(
            [held[s].reshape(4 * K, W) for s in range(first, last)], axis=1
        )
        for t in range(RT):
            share = jnp.dot(lhs, hot[t, first * W : last * W, :], preferred_element_type=F32)
            if first > 0:
                share = share + spread[t]
            if last < NZ:
                spread[t] = share
            else:
                which = jnp.broadcast_to(high[t], (K, B))
                picked = share[:K]
                for i in range(1, 4):
                    picked = jnp.where(which == i, share[i * K : (i + 1) * K], picked)
                xs[t] = picked.astype(BF16)

    for load in loads:
        load.wait()
    rank_row = lax.broadcasted_iota(jnp.int32, (R, K), 0)
    for t in range(RT):
        value = lax.dot_general(
            left[t].reshape(CT * R, B), xs[t], (((1,), (1,)), ((), ())),
            preferred_element_type=F32,
        )
        for c in range(CT):
            keep = rank_row < rank_ref[c, t]
            proj[t, c] = jnp.where(keep, value[c * R : (c + 1) * R], 0.0).astype(BF16)

    products = []
    for n in range(SLOTS):
        lhs = xs[index_ref[0, n]]
        products.append(jnp.dot(lhs, near[n], preferred_element_type=F32))

    def column_tile(c):
        total = lax.dot_general(
            proj[:, c].reshape(RT * R, K), right[:, c].reshape(RT * R, B),
            (((0,), (0,)), ((), ())), preferred_element_type=F32,
        )
        for n in range(SLOTS):
            used = jnp.logical_and(index_ref[1, n] == c, n < count_ref[0, 0])
            total = total + jnp.where(used, products[n], 0.0)
        return total

    for d in (2, 1, 3, 0):
        to = (x + d) % NX
        for j in range(2):
            total = column_tile(to * 2 + j)
            for i in range(2):
                half = total[:, i * W : (i + 1) * W]
                if d == 0:
                    acc[2 * j + i] = half
                else:
                    sbuf[d - 1, 2 * j + i] = half.astype(BF16)

    xcopy, vcopy = {}, {}
    for e in (2, 1, 3, 0):
        for d in (2, 1, 3):
            xcopy[d, e] = send(
                sbuf.at[d - 1, (v + e) % NY], xbuf.at[d - 1, e],
                xsend.at[d - 1, e], xrecv.at[d - 1, e], "row", xpeers[d - 1],
            )

    def row_sum(e):
        total = acc[(v + e) % NY]
        for d in (1, 3, 2):
            xcopy[d, e].wait_recv()
        for d in (1, 3, 2):
            total = total + xbuf[d - 1, e].astype(F32)
        return total

    for e in (2, 1, 3):
        encode(row_sum(e), vbuf.at[e - 1])
        vcopy[e] = send(
            vbuf.at[e - 1], ybuf.at[e - 1], vsend.at[e - 1], vrecv.at[e - 1],
            "row", vpeers[e - 1],
        )
    total = row_sum(0)
    for e in (1, 3, 2):
        vcopy[e].wait_recv()
        total = total + decode(ybuf.at[e - 1])
    out_ref[...] = total
    for copy in copies:
        copy.wait_send()


def local(
    adjoint, panel_order, left_factor, right_factor, tile_ranks, near_blocks, near_index, near_count
):
    vmem = pl.BlockSpec(memory_space=pltpu.VMEM)
    smem = pl.BlockSpec(memory_space=pltpu.SMEM)
    hbm = pl.BlockSpec(memory_space=pl.ANY)
    dma = pltpu.SemaphoreType.DMA
    return pl.pallas_call(
        kernel,
        out_shape=jax.ShapeDtypeStruct((K, W), F32),
        in_specs=[hbm, smem, hbm, hbm, hbm, hbm, hbm, hbm],
        out_specs=vmem,
        scratch_shapes=[
            pltpu.SMEM((2, SLOTS), jnp.int32),
            pltpu.SMEM((CT, RT), jnp.int32),
            pltpu.VMEM((RT, 1, B), jnp.int32),
            pltpu.VMEM((K, W), BF16),
            pltpu.VMEM((RT, CT, R, B), BF16),
            pltpu.VMEM((RT, CT, R, B), BF16),
            pltpu.VMEM((SLOTS, B, B), BF16),
            pltpu.VMEM((RT, NZ * W, B), BF16),
            pltpu.VMEM((RT, 1, B), jnp.int32),
            pltpu.VMEM((NZ, 4, K, W), BF16),
            pltpu.VMEM((RT, 4 * K, B), F32),
            pltpu.VMEM((RT, K, B), BF16),
            pltpu.VMEM((RT, CT, R, K), BF16),
            pltpu.VMEM((NX - 1, NY, K, W), BF16),
            pltpu.VMEM((NX - 1, NY, K, W), BF16),
            pltpu.VMEM((NY, K, W), F32),
            pltpu.VMEM((NY - 1, K + 16, W), jnp.int16),
            pltpu.VMEM((NY - 1, K + 16, W), jnp.int16),
            dma((7,)), dma((7,)), dma((7,)), dma((8,)), dma((8,)), dma((8,)), dma((8,)),
            dma((8,)), dma((8,)), dma((3, 4)), dma((3, 4)), dma((3,)), dma((3,)),
        ],
        compiler_params=pltpu.CompilerParams(
            collective_id=0, has_side_effects=True, vmem_limit_bytes=60 << 20
        ),
    )(
        near_index[0, 0], near_count, tile_ranks.T, panel_order.reshape(RT, 1, B), adjoint,
        left_factor, right_factor, near_blocks[0, 0],
    )


def solution(mesh):
    placed = (
        P(None, ("row", "col")),
        P("row", None),
        P("row", "col", None, None),
        P("row", "col", None, None),
        P("row", "col"),
        P("row", "col", None, None, None),
        P("row", "col", None, None),
        P("row", "col"),
    )
    return jax.shard_map(
        local, mesh=mesh, in_specs=placed, out_specs=P(None, ("col", "row")), check_vma=False
    )
```

```python
import jax
import jax.numpy as jnp
from jax import lax
from jax.experimental import pallas as pl
from jax.experimental.pallas import tpu as pltpu
from jax.sharding import PartitionSpec as P

MESH = pl.DeviceIdType.MESH
F32 = jnp.float32
BF16 = jnp.bfloat16

NZ = 8
NX = 4
NY = 4
K = 64
B = 256
W = 128
RT = 16
CT = 8
R = 16
SLOTS = 8

ARRIVAL = (0, 1, 7, 2, 6, 3, 5, 4)
SLOT = {d: s for s, d in enumerate(ARRIVAL)}
RELAYS = {0: (2, 6, 1, 7), 2: (2, 1), 6: (7,)}
CHUNKS = ((0, 4), (4, 6), (6, 8))


def encode(value, ref):
    groups = value.reshape(8, 8, W)
    most = jnp.maximum(jnp.max(jnp.abs(groups), axis=0), 1e-30)
    power = jnp.floor(jnp.log2(most))
    coded = jnp.round(groups * jnp.exp2(13.0 - power)[None]).reshape(K, W)
    ref[:K] = coded.astype(jnp.int32).astype(jnp.int16)
    power = power.astype(jnp.int32)
    ref[K:] = jnp.concatenate([power, power], axis=0).astype(jnp.int16)


def decode(ref):
    power = ref[K:].astype(jnp.int32)[:8].astype(F32)
    groups = ref[:K].astype(jnp.int32).astype(F32).reshape(8, 8, W)
    return (groups * jnp.exp2(power - 13.0)[None]).reshape(K, W)


def kernel(
    index_hbm, count_ref, rank_hbm, order_hbm, a_hbm, left_hbm, right_hbm, near_hbm, out_ref,
    index_ref, rank_ref, order_ref, own, left, right, near, hot, high, held, spread, xs, proj,
    sbuf, xbuf, acc, vbuf, ybuf,
    load_sem, zsend, zrecv, ysend, yrecv, csend, crecv, dsend, drecv, xsend, xrecv, vsend, vrecv, beside_sem,
):
    g = lax.axis_index("row")
    h = lax.axis_index("col")
    z, part = h // 4, h % 4
    x, v = g // NY, g % NY
    cpeer = z * 4 + part + 1 - 2 * (part % 2)
    ypeer = z * 4 + (part + 2) % 4
    dpeer = z * 4 + 3 - part
    zpeers = [((z + d) % NZ) * 4 + part for d in range(1, NZ)]
    xpeers = [((x + d) % NX) * NY + v for d in range(1, NX)]
    vpeers = [x * NY + (v + d) % NY for d in range(1, NY)]

    mine, ordering, *loads = [
        pltpu.make_async_copy(src, dst, load_sem.at[i])
        for i, (src, dst) in enumerate((
            (a_hbm, own), (order_hbm, order_ref), (left_hbm, left), (right_hbm, right),
            (near_hbm, near), (rank_hbm, rank_ref), (index_hbm, index_ref),
        ))
    ]
    mine.start()
    ordering.start()

    barrier = pltpu.get_barrier_semaphore()
    for peer in (*(zpeers[d - 1] for d in RELAYS[0]), ypeer, cpeer, dpeer):
        pl.semaphore_signal(barrier, inc=1, device_id={"col": peer}, device_id_type=MESH)
    beside = (xpeers[0], xpeers[2], vpeers[0], vpeers[2])
    for peer in beside:
        pl.semaphore_signal(barrier, inc=1, device_id={"row": peer}, device_id_type=MESH)
    pl.semaphore_wait(barrier, len(RELAYS[0]) + 3 + len(beside))
    mine.wait()

    copies = []

    def send(src, dst, ssem, rsem, axis, peer):
        copy = pltpu.make_async_remote_copy(
            src_ref=src, dst_ref=dst, send_sem=ssem, recv_sem=rsem,
            device_id={axis: peer}, device_id_type=MESH,
        )
        copy.start()
        copies.append(copy)
        return copy

    zcopy, ycopy, ccopy, dcopy = {}, {}, {}, {}

    def pass_on(d, steps):
        block = held.at[SLOT[d], 0] if d else own
        for step in steps:
            to = (d + step) % NZ
            zcopy[to] = send(
                block, held.at[SLOT[to], 0], zsend.at[to - 1], zrecv.at[to - 1],
                "col", zpeers[step - 1],
            )

    def forward(d):
        block = held.at[SLOT[d], 0] if d else own
        s = SLOT[d]
        ycopy[d] = send(block, held.at[s, 2], ysend.at[s], yrecv.at[s], "col", ypeer)
        dcopy[d] = send(block, held.at[s, 3], dsend.at[s], drecv.at[s], "col", dpeer)
        ccopy[d] = send(block, held.at[s, 1], csend.at[s], crecv.at[s], "col", cpeer)

    pass_on(0, RELAYS[0])
    forward(0)
    for peer in beside:
        pl.semaphore_signal(beside_sem, inc=1, device_id={"row": peer}, device_id_type=MESH)
    for load in loads:
        load.start()
    held[0, 0] = own[...]

    ordering.wait()

    def build(t, carry):
        source = order_ref[t]
        device = source // W
        dz = lax.rem(z + NZ - device // 4, NZ)
        slot = jnp.where(dz <= 4, jnp.maximum(2 * dz - 1, 0), 16 - 2 * dz)
        high[t] = lax.rem(device, 4) ^ part
        low = jnp.broadcast_to(slot * W + lax.rem(source, W), (R, B)).astype(jnp.int16)
        row = lax.broadcasted_iota(jnp.int32, (R, B), 0).astype(jnp.int16)
        one, zero = jnp.ones((R, B), BF16), jnp.zeros((R, B), BF16)
        for i in range(NZ * W // R):
            hot[t, i * R : (i + 1) * R, :] = jnp.where(low == row + jnp.int16(i * R), one, zero)
        return carry

    lax.fori_loop(0, RT, build, 0)

    for d in (2, 6, 1, 7, 3, 5, 4):
        zcopy[d].wait_recv()
        pass_on(d, RELAYS.get(d, ()))
        forward(d)

    for first, last in CHUNKS:
        for d in ARRIVAL[first:last]:
            ycopy[d].wait_recv()
            ccopy[d].wait_recv()
            dcopy[d].wait_recv()
        lhs = jnp.concatenate(
            [held[s].reshape(4 * K, W) for s in range(first, last)], axis=1
        )
        for t in range(RT):
            share = jnp.dot(lhs, hot[t, first * W : last * W, :], preferred_element_type=F32)
            if first > 0:
                share = share + spread[t]
            if last < NZ:
                spread[t] = share
            else:
                which = jnp.broadcast_to(high[t], (K, B))
                picked = share[:K]
                for i in range(1, 4):
                    picked = jnp.where(which == i, share[i * K : (i + 1) * K], picked)
                xs[t] = picked.astype(BF16)

    for load in loads:
        load.wait()
    rank_row = lax.broadcasted_iota(jnp.int32, (R, K), 0)
    for t in range(RT):
        value = lax.dot_general(
            left[t].reshape(CT * R, B), xs[t], (((1,), (1,)), ((), ())),
            preferred_element_type=F32,
        )
        for c in range(CT):
            keep = rank_row < rank_ref[c, t]
            proj[t, c] = jnp.where(keep, value[c * R : (c + 1) * R], 0.0).astype(BF16)

    products = []
    for n in range(SLOTS):
        lhs = xs[index_ref[0, n]]
        products.append(jnp.dot(lhs, near[n], preferred_element_type=F32))

    def column_tile(c):
        total = lax.dot_general(
            proj[:, c].reshape(RT * R, K), right[:, c].reshape(RT * R, B),
            (((0,), (0,)), ((), ())), preferred_element_type=F32,
        )
        for n in range(SLOTS):
            used = jnp.logical_and(index_ref[1, n] == c, n < count_ref[0, 0])
            total = total + jnp.where(used, products[n], 0.0)
        return total

    for d in (2, 1, 3, 0):
        to = (x + d) % NX
        for j in range(2):
            total = column_tile(to * 2 + j)
            for i in range(2):
                half = total[:, i * W : (i + 1) * W]
                if d == 0:
                    acc[2 * j + i] = half
                else:
                    sbuf[d - 1, 2 * j + i] = half.astype(BF16)

    pl.semaphore_wait(beside_sem, len(beside))
    xcopy, vcopy = {}, {}
    for e in (2, 1, 3, 0):
        for d in (2, 1, 3):
            xcopy[d, e] = send(
                sbuf.at[d - 1, (v + e) % NY], xbuf.at[d - 1, e],
                xsend.at[d - 1, e], xrecv.at[d - 1, e], "row", xpeers[d - 1],
            )

    def row_sum(e):
        total = acc[(v + e) % NY]
        for d in (1, 3, 2):
            xcopy[d, e].wait_recv()
        for d in (1, 3, 2):
            total = total + xbuf[d - 1, e].astype(F32)
        return total

    for e in (2, 1, 3):
        encode(row_sum(e), vbuf.at[e - 1])
        vcopy[e] = send(
            vbuf.at[e - 1], ybuf.at[e - 1], vsend.at[e - 1], vrecv.at[e - 1],
            "row", vpeers[e - 1],
        )
    total = row_sum(0)
    for e in (1, 3, 2):
        vcopy[e].wait_recv()
        total = total + decode(ybuf.at[e - 1])
    out_ref[...] = total
    for copy in copies:
        copy.wait_send()


def local(
    adjoint, panel_order, left_factor, right_factor, tile_ranks, near_blocks, near_index, near_count
):
    vmem = pl.BlockSpec(memory_space=pltpu.VMEM)
    smem = pl.BlockSpec(memory_space=pltpu.SMEM)
    hbm = pl.BlockSpec(memory_space=pl.ANY)
    dma = pltpu.SemaphoreType.DMA
    return pl.pallas_call(
        kernel,
        out_shape=jax.ShapeDtypeStruct((K, W), F32),
        in_specs=[hbm, smem, hbm, hbm, hbm, hbm, hbm, hbm],
        out_specs=vmem,
        scratch_shapes=[
            pltpu.SMEM((2, SLOTS), jnp.int32),
            pltpu.SMEM((CT, RT), jnp.int32),
            pltpu.VMEM((RT, 1, B), jnp.int32),
            pltpu.VMEM((K, W), BF16),
            pltpu.VMEM((RT, CT, R, B), BF16),
            pltpu.VMEM((RT, CT, R, B), BF16),
            pltpu.VMEM((SLOTS, B, B), BF16),
            pltpu.VMEM((RT, NZ * W, B), BF16),
            pltpu.VMEM((RT, 1, B), jnp.int32),
            pltpu.VMEM((NZ, 4, K, W), BF16),
            pltpu.VMEM((RT, 4 * K, B), F32),
            pltpu.VMEM((RT, K, B), BF16),
            pltpu.VMEM((RT, CT, R, K), BF16),
            pltpu.VMEM((NX - 1, NY, K, W), BF16),
            pltpu.VMEM((NX - 1, NY, K, W), BF16),
            pltpu.VMEM((NY, K, W), F32),
            pltpu.VMEM((NY - 1, K + 16, W), jnp.int16),
            pltpu.VMEM((NY - 1, K + 16, W), jnp.int16),
            dma((7,)), dma((7,)), dma((7,)), dma((8,)), dma((8,)), dma((8,)), dma((8,)),
            dma((8,)), dma((8,)), dma((3, 4)), dma((3, 4)), dma((3,)), dma((3,)),
            pltpu.SemaphoreType.REGULAR,
        ],
        compiler_params=pltpu.CompilerParams(
            collective_id=0, has_side_effects=True, vmem_limit_bytes=60 << 20
        ),
    )(
        near_index[0, 0], near_count, tile_ranks.T, panel_order.reshape(RT, 1, B), adjoint,
        left_factor, right_factor, near_blocks[0, 0],
    )


def solution(mesh):
    placed = (
        P(None, ("row", "col")),
        P("row", None),
        P("row", "col", None, None),
        P("row", "col", None, None),
        P("row", "col"),
        P("row", "col", None, None, None),
        P("row", "col", None, None),
        P("row", "col"),
    )
    return jax.shard_map(
        local, mesh=mesh, in_specs=placed, out_specs=P(None, ("col", "row")), check_vma=False
    )
```

```python
import jax
import jax.numpy as jnp
from jax import lax
from jax.experimental import pallas as pl
from jax.experimental.pallas import tpu as pltpu
from jax.sharding import PartitionSpec as P

MESH = pl.DeviceIdType.MESH
F32 = jnp.float32
BF16 = jnp.bfloat16

NZ = 8
NX = 4
NY = 4
K = 64
B = 256
W = 128
RT = 16
CT = 8
R = 16
SLOTS = 8

ARRIVAL = (0, 1, 7, 2, 6, 3, 5, 4)
SLOT = {d: s for s, d in enumerate(ARRIVAL)}
RELAYS = {0: (2, 6, 1, 7), 2: (2, 1), 6: (7,)}
CHUNKS = ((0, 4), (4, 6), (6, 8))


def encode(value, ref):
    groups = value.reshape(8, 8, W)
    most = jnp.maximum(jnp.max(jnp.abs(groups), axis=0), 1e-30)
    power = jnp.floor(jnp.log2(most))
    coded = jnp.round(groups * jnp.exp2(13.0 - power)[None]).reshape(K, W)
    ref[:K] = coded.astype(jnp.int32).astype(jnp.int16)
    power = power.astype(jnp.int32)
    ref[K:] = jnp.concatenate([power, power], axis=0).astype(jnp.int16)


def decode(ref):
    power = ref[K:].astype(jnp.int32)[:8].astype(F32)
    groups = ref[:K].astype(jnp.int32).astype(F32).reshape(8, 8, W)
    return (groups * jnp.exp2(power - 13.0)[None]).reshape(K, W)


def kernel(
    index_hbm, count_ref, rank_hbm, order_hbm, a_hbm, left_hbm, right_hbm, near_hbm, out_ref,
    index_ref, rank_ref, order_ref, own, left, right, near, hot, high, held, spread, xs, proj,
    sbuf, xbuf, acc, vbuf, ybuf,
    load_sem, zsend, zrecv, ysend, yrecv, csend, crecv, dsend, drecv, xsend, xrecv, vsend, vrecv, beside_sem,
):
    g = lax.axis_index("row")
    h = lax.axis_index("col")
    z, part = h // 4, h % 4
    x, v = g // NY, g % NY
    cpeer = z * 4 + part + 1 - 2 * (part % 2)
    ypeer = z * 4 + (part + 2) % 4
    dpeer = z * 4 + 3 - part
    zpeers = [((z + d) % NZ) * 4 + part for d in range(1, NZ)]
    xpeers = [((x + d) % NX) * NY + v for d in range(1, NX)]
    vpeers = [x * NY + (v + d) % NY for d in range(1, NY)]

    mine, ordering, *loads = [
        pltpu.make_async_copy(src, dst, load_sem.at[i])
        for i, (src, dst) in enumerate((
            (a_hbm, own), (order_hbm, order_ref), (left_hbm, left), (right_hbm, right),
            (near_hbm, near), (rank_hbm, rank_ref), (index_hbm, index_ref),
        ))
    ]
    mine.start()
    ordering.start()

    barrier = pltpu.get_barrier_semaphore()
    for peer in (*(zpeers[d - 1] for d in RELAYS[0]), ypeer, cpeer, dpeer):
        pl.semaphore_signal(barrier, inc=1, device_id={"col": peer}, device_id_type=MESH)
    beside = (xpeers[0], xpeers[2], vpeers[0], vpeers[2])
    for peer in beside:
        pl.semaphore_signal(barrier, inc=1, device_id={"row": peer}, device_id_type=MESH)
    pl.semaphore_wait(barrier, len(RELAYS[0]) + 3 + len(beside))
    mine.wait()

    copies = []

    def send(src, dst, ssem, rsem, axis, peer):
        copy = pltpu.make_async_remote_copy(
            src_ref=src, dst_ref=dst, send_sem=ssem, recv_sem=rsem,
            device_id={axis: peer}, device_id_type=MESH,
        )
        copy.start()
        copies.append(copy)
        return copy

    zcopy, ycopy, ccopy, dcopy = {}, {}, {}, {}

    def pass_on(d, steps):
        block = held.at[SLOT[d], 0] if d else own
        for step in steps:
            to = (d + step) % NZ
            zcopy[to] = send(
                block, held.at[SLOT[to], 0], zsend.at[to - 1], zrecv.at[to - 1],
                "col", zpeers[step - 1],
            )

    def forward(d):
        block = held.at[SLOT[d], 0] if d else own
        s = SLOT[d]
        ycopy[d] = send(block, held.at[s, 2], ysend.at[s], yrecv.at[s], "col", ypeer)
        dcopy[d] = send(block, held.at[s, 3], dsend.at[s], drecv.at[s], "col", dpeer)
        ccopy[d] = send(block, held.at[s, 1], csend.at[s], crecv.at[s], "col", cpeer)

    pass_on(0, RELAYS[0])
    forward(0)
    for peer in beside:
        pl.semaphore_signal(beside_sem, inc=1, device_id={"row": peer}, device_id_type=MESH)
    for load in loads:
        load.start()
    held[0, 0] = own[...]

    ordering.wait()

    def build(t, carry):
        source = order_ref[t]
        device = source // W
        dz = lax.rem(z + NZ - device // 4, NZ)
        slot = jnp.where(dz <= 4, jnp.maximum(2 * dz - 1, 0), 16 - 2 * dz)
        high[t] = lax.rem(device, 4) ^ part
        low = jnp.broadcast_to(slot * W + lax.rem(source, W), (R, B)).astype(jnp.int16)
        row = lax.broadcasted_iota(jnp.int32, (R, B), 0).astype(jnp.int16)
        one, zero = jnp.ones((R, B), BF16), jnp.zeros((R, B), BF16)
        for i in range(NZ * W // R):
            hot[t, i * R : (i + 1) * R, :] = jnp.where(low == row + jnp.int16(i * R), one, zero)
        return carry

    lax.fori_loop(0, RT, build, 0)

    for d in (2, 6, 1, 7, 3, 5, 4):
        zcopy[d].wait_recv()
        pass_on(d, RELAYS.get(d, ()))
        forward(d)

    for first, last in CHUNKS:
        for d in ARRIVAL[first:last]:
            ycopy[d].wait_recv()
            ccopy[d].wait_recv()
            dcopy[d].wait_recv()
        lhs = jnp.concatenate(
            [held[s].reshape(4 * K, W) for s in range(first, last)], axis=1
        )
        for t in range(RT):
            share = jnp.dot(lhs, hot[t, first * W : last * W, :], preferred_element_type=F32)
            if first > 0:
                share = share + spread[t]
            if last < NZ:
                spread[t] = share
            else:
                which = jnp.broadcast_to(high[t], (K, B))
                picked = share[:K]
                for i in range(1, 4):
                    picked = jnp.where(which == i, share[i * K : (i + 1) * K], picked)
                xs[t] = picked.astype(BF16)

    for load in loads:
        load.wait()
    rank_row = lax.broadcasted_iota(jnp.int32, (R, K), 0)
    for t in range(RT):
        value = lax.dot_general(
            left[t].reshape(CT * R, B), xs[t], (((1,), (1,)), ((), ())),
            preferred_element_type=F32,
        )
        for c in range(CT):
            keep = rank_row < rank_ref[c, t]
            proj[t, c] = jnp.where(keep, value[c * R : (c + 1) * R], 0.0).astype(BF16)

    products = []
    for n in range(SLOTS):
        lhs = xs[index_ref[0, n]]
        products.append(jnp.dot(lhs, near[n], preferred_element_type=F32))

    def column_tile(c):
        total = lax.dot_general(
            proj[:, c].reshape(RT * R, K), right[:, c].reshape(RT * R, B),
            (((0,), (0,)), ((), ())), preferred_element_type=F32,
        )
        for n in range(SLOTS):
            used = jnp.logical_and(index_ref[1, n] == c, n < count_ref[0, 0])
            total = total + jnp.where(used, products[n], 0.0)
        return total

    for d in (2, 1, 3, 0):
        to = (x + d) % NX
        for j in range(2):
            total = column_tile(to * 2 + j)
            for i in range(2):
                half = total[:, i * W : (i + 1) * W]
                if d == 0:
                    acc[2 * j + i] = half
                else:
                    sbuf[d - 1, 2 * j + i] = half.astype(BF16)

    pl.semaphore_wait(beside_sem, len(beside))
    xcopy, vcopy = {}, {}
    for e in (2, 1, 3, 0):
        for d in (2, 1, 3):
            xcopy[d, e] = send(
                sbuf.at[d - 1, (v + e) % NY], xbuf.at[d - 1, e],
                xsend.at[d - 1, e], xrecv.at[d - 1, e], "row", xpeers[d - 1],
            )

    def row_sum(e):
        total = acc[(v + e) % NY]
        for d in (1, 3, 2):
            xcopy[d, e].wait_recv()
        for d in (1, 3, 2):
            total = total + xbuf[d - 1, e].astype(F32)
        return total

    for e in (2, 1, 3):
        encode(row_sum(e), vbuf.at[e - 1])
        vcopy[e] = send(
            vbuf.at[e - 1], ybuf.at[e - 1], vsend.at[e - 1], vrecv.at[e - 1],
            "row", vpeers[e - 1],
        )
    total = row_sum(0)
    for e in (1, 3, 2):
        vcopy[e].wait_recv()
        total = total + decode(ybuf.at[e - 1])
    out_ref[...] = total
    for copy in copies:
        copy.wait_send()


def local(
    adjoint, panel_order, left_factor, right_factor, tile_ranks, near_blocks, near_index, near_count
):
    vmem = pl.BlockSpec(memory_space=pltpu.VMEM)
    smem = pl.BlockSpec(memory_space=pltpu.SMEM)
    hbm = pl.BlockSpec(memory_space=pl.ANY)
    dma = pltpu.SemaphoreType.DMA
    return pl.pallas_call(
        kernel,
        out_shape=pltpu.VMEM((K, W), F32),
        in_specs=[hbm, smem, hbm, hbm, hbm, hbm, hbm, hbm],
        out_specs=vmem,
        scratch_shapes=[
            pltpu.SMEM((2, SLOTS), jnp.int32),
            pltpu.SMEM((CT, RT), jnp.int32),
            pltpu.VMEM((RT, 1, B), jnp.int32),
            pltpu.VMEM((K, W), BF16),
            pltpu.VMEM((RT, CT, R, B), BF16),
            pltpu.VMEM((RT, CT, R, B), BF16),
            pltpu.VMEM((SLOTS, B, B), BF16),
            pltpu.VMEM((RT, NZ * W, B), BF16),
            pltpu.VMEM((RT, 1, B), jnp.int32),
            pltpu.VMEM((NZ, 4, K, W), BF16),
            pltpu.VMEM((RT, 4 * K, B), F32),
            pltpu.VMEM((RT, K, B), BF16),
            pltpu.VMEM((RT, CT, R, K), BF16),
            pltpu.VMEM((NX - 1, NY, K, W), BF16),
            pltpu.VMEM((NX - 1, NY, K, W), BF16),
            pltpu.VMEM((NY, K, W), F32),
            pltpu.VMEM((NY - 1, K + 16, W), jnp.int16),
            pltpu.VMEM((NY - 1, K + 16, W), jnp.int16),
            dma((7,)), dma((7,)), dma((7,)), dma((8,)), dma((8,)), dma((8,)), dma((8,)),
            dma((8,)), dma((8,)), dma((3, 4)), dma((3, 4)), dma((3,)), dma((3,)),
            pltpu.SemaphoreType.REGULAR,
        ],
        compiler_params=pltpu.CompilerParams(
            collective_id=0, has_side_effects=True, vmem_limit_bytes=60 << 20
        ),
    )(
        near_index[0, 0], near_count, tile_ranks.T, panel_order.reshape(RT, 1, B), adjoint,
        left_factor, right_factor, near_blocks[0, 0],
    )


def solution(mesh):
    placed = (
        P(None, ("row", "col")),
        P("row", None),
        P("row", "col", None, None),
        P("row", "col", None, None),
        P("row", "col"),
        P("row", "col", None, None, None),
        P("row", "col", None, None),
        P("row", "col"),
    )
    return jax.shard_map(
        local, mesh=mesh, in_specs=placed, out_specs=P(None, ("col", "row")), check_vma=False
    )
```

```python
import jax
import jax.numpy as jnp
from jax import lax
from jax.experimental import pallas as pl
from jax.experimental.pallas import tpu as pltpu
from jax.sharding import PartitionSpec as P

MESH = pl.DeviceIdType.MESH
F32 = jnp.float32
BF16 = jnp.bfloat16

NZ = 8
NX = 4
NY = 4
K = 64
B = 256
W = 128
RT = 16
CT = 8
R = 16
SLOTS = 8

ARRIVAL = (0, 1, 7, 2, 6, 3, 5, 4)
SLOT = {d: s for s, d in enumerate(ARRIVAL)}
RELAYS = {0: (2, 6, 1, 7), 2: (2, 1), 6: (7,)}
CHUNKS = ((0, 4), (4, 6), (6, 8))


def encode(value, ref):
    groups = value.reshape(8, 8, W)
    most = jnp.maximum(jnp.max(jnp.abs(groups), axis=0), 1e-30)
    power = jnp.floor(jnp.log2(most))
    coded = jnp.round(groups * jnp.exp2(13.0 - power)[None]).reshape(K, W)
    ref[:K] = coded.astype(jnp.int32).astype(jnp.int16)
    power = power.astype(jnp.int32)
    ref[K:] = jnp.concatenate([power, power], axis=0).astype(jnp.int16)


def decode(ref):
    power = ref[K:].astype(jnp.int32)[:8].astype(F32)
    groups = ref[:K].astype(jnp.int32).astype(F32).reshape(8, 8, W)
    return (groups * jnp.exp2(power - 13.0)[None]).reshape(K, W)


def kernel(
    index_hbm, count_ref, rank_hbm, order_hbm, a_hbm, left_hbm, right_hbm, near_hbm, out_ref,
    index_ref, rank_ref, order_ref, own, left, right, near, hot, high, held, spread, xs, proj,
    sbuf, xbuf, acc, vbuf, ybuf,
    load_sem, zsend, zrecv, ysend, yrecv, csend, crecv, dsend, drecv, xsend, xrecv, vsend, vrecv, beside_sem,
):
    g = lax.axis_index("row")
    h = lax.axis_index("col")
    z, part = h // 4, h % 4
    x, v = g // NY, g % NY
    cpeer = z * 4 + part + 1 - 2 * (part % 2)
    ypeer = z * 4 + (part + 2) % 4
    dpeer = z * 4 + 3 - part
    zpeers = [((z + d) % NZ) * 4 + part for d in range(1, NZ)]
    xpeers = [((x + d) % NX) * NY + v for d in range(1, NX)]
    vpeers = [x * NY + (v + d) % NY for d in range(1, NY)]

    mine, ordering, *loads = [
        pltpu.make_async_copy(src, dst, load_sem.at[i])
        for i, (src, dst) in enumerate((
            (a_hbm, own), (order_hbm, order_ref), (left_hbm, left), (right_hbm, right),
            (near_hbm, near), (rank_hbm, rank_ref), (index_hbm, index_ref),
        ))
    ]
    mine.start()
    ordering.start()

    barrier = pltpu.get_barrier_semaphore()
    for peer in (*(zpeers[d - 1] for d in RELAYS[0]), ypeer, cpeer, dpeer):
        pl.semaphore_signal(barrier, inc=1, device_id={"col": peer}, device_id_type=MESH)
    beside = (xpeers[0], xpeers[2], vpeers[0], vpeers[2])
    for peer in beside:
        pl.semaphore_signal(barrier, inc=1, device_id={"row": peer}, device_id_type=MESH)
    pl.semaphore_wait(barrier, len(RELAYS[0]) + 3 + len(beside))
    mine.wait()

    copies = []

    def send(src, dst, ssem, rsem, axis, peer):
        copy = pltpu.make_async_remote_copy(
            src_ref=src, dst_ref=dst, send_sem=ssem, recv_sem=rsem,
            device_id={axis: peer}, device_id_type=MESH,
        )
        copy.start()
        copies.append(copy)
        return copy

    zcopy, ycopy, ccopy, dcopy = {}, {}, {}, {}

    def pass_on(d, steps):
        block = held.at[SLOT[d], 0] if d else own
        for step in steps:
            to = (d + step) % NZ
            zcopy[to] = send(
                block, held.at[SLOT[to], 0], zsend.at[to - 1], zrecv.at[to - 1],
                "col", zpeers[step - 1],
            )

    def forward(d):
        block = held.at[SLOT[d], 0] if d else own
        s = SLOT[d]
        ycopy[d] = send(block, held.at[s, 2], ysend.at[s], yrecv.at[s], "col", ypeer)
        dcopy[d] = send(block, held.at[s, 3], dsend.at[s], drecv.at[s], "col", dpeer)
        ccopy[d] = send(block, held.at[s, 1], csend.at[s], crecv.at[s], "col", cpeer)

    pass_on(0, RELAYS[0])
    forward(0)
    for peer in beside:
        pl.semaphore_signal(beside_sem, inc=1, device_id={"row": peer}, device_id_type=MESH)
    for load in loads:
        load.start()
    held[0, 0] = own[...]

    ordering.wait()

    def build(t, carry):
        source = order_ref[t]
        device = source // W
        dz = lax.rem(z + NZ - device // 4, NZ)
        slot = jnp.where(dz <= 4, jnp.maximum(2 * dz - 1, 0), 16 - 2 * dz)
        high[t] = lax.rem(device, 4) ^ part
        low = jnp.broadcast_to(slot * W + lax.rem(source, W), (R, B)).astype(jnp.int16)
        row = lax.broadcasted_iota(jnp.int32, (R, B), 0).astype(jnp.int16)
        one, zero = jnp.ones((R, B), BF16), jnp.zeros((R, B), BF16)
        for i in range(NZ * W // R):
            hot[t, i * R : (i + 1) * R, :] = jnp.where(low == row + jnp.int16(i * R), one, zero)
        return carry

    lax.fori_loop(0, RT, build, 0)

    for d in (2, 6, 1, 7, 3, 5, 4):
        zcopy[d].wait_recv()
        pass_on(d, RELAYS.get(d, ()))
        forward(d)

    for load in loads:
        load.wait()
    row = lax.broadcasted_iota(jnp.int32, (R, B), 0)
    for t in range(RT):
        for c in range(CT):
            left[t, c] = jnp.where(row < rank_ref[c, t], left[t, c].astype(F32), 0.0).astype(BF16)

    for first, last in CHUNKS:
        for d in ARRIVAL[first:last]:
            ycopy[d].wait_recv()
            ccopy[d].wait_recv()
            dcopy[d].wait_recv()
        lhs = jnp.concatenate(
            [held[s].reshape(4 * K, W) for s in range(first, last)], axis=1
        )
        for t in range(RT):
            share = jnp.dot(lhs, hot[t, first * W : last * W, :], preferred_element_type=F32)
            if first > 0:
                share = share + spread[t]
            if last < NZ:
                spread[t] = share
            else:
                which = jnp.broadcast_to(high[t], (K, B))
                picked = share[:K]
                for i in range(1, 4):
                    picked = jnp.where(which == i, share[i * K : (i + 1) * K], picked)
                xs[t] = picked.astype(BF16)

    for t in range(RT):
        value = lax.dot_general(
            left[t].reshape(CT * R, B), xs[t], (((1,), (1,)), ((), ())),
            preferred_element_type=F32,
        )
        proj[t] = value.astype(BF16).reshape(CT, R, K)

    products = []
    for n in range(SLOTS):
        lhs = xs[index_ref[0, n]]
        products.append(jnp.dot(lhs, near[n], preferred_element_type=F32))

    def column_tile(c):
        total = lax.dot_general(
            proj[:, c].reshape(RT * R, K), right[:, c].reshape(RT * R, B),
            (((0,), (0,)), ((), ())), preferred_element_type=F32,
        )
        for n in range(SLOTS):
            used = jnp.logical_and(index_ref[1, n] == c, n < count_ref[0, 0])
            total = total + jnp.where(used, products[n], 0.0)
        return total

    def share(d):
        to = (x + d) % NX
        for j in range(2):
            total = column_tile(to * 2 + j)
            for i in range(2):
                half = total[:, i * W : (i + 1) * W]
                if d == 0:
                    acc[2 * j + i] = half
                else:
                    sbuf[d - 1, 2 * j + i] = half.astype(BF16)

    for d in (2, 1, 3):
        share(d)

    pl.semaphore_wait(beside_sem, len(beside))
    xcopy, vcopy = {}, {}
    for e in (2, 1, 3, 0):
        for d in (2, 1, 3):
            xcopy[d, e] = send(
                sbuf.at[d - 1, (v + e) % NY], xbuf.at[d - 1, e],
                xsend.at[d - 1, e], xrecv.at[d - 1, e], "row", xpeers[d - 1],
            )

    share(0)
    for copy in copies[:-12]:
        copy.wait_send()

    def row_sum(e):
        total = acc[(v + e) % NY]
        for d in (1, 3, 2):
            xcopy[d, e].wait_recv()
        for d in (1, 3, 2):
            total = total + xbuf[d - 1, e].astype(F32)
        return total

    for e in (2, 1, 3):
        encode(row_sum(e), vbuf.at[e - 1])
        vcopy[e] = send(
            vbuf.at[e - 1], ybuf.at[e - 1], vsend.at[e - 1], vrecv.at[e - 1],
            "row", vpeers[e - 1],
        )
    total = row_sum(0)
    for copy in xcopy.values():
        copy.wait_send()
    for e in (1, 3, 2):
        vcopy[e].wait_recv()
        total = total + decode(ybuf.at[e - 1])
    out_ref[...] = total
    for copy in vcopy.values():
        copy.wait_send()


def local(
    adjoint, panel_order, left_factor, right_factor, tile_ranks, near_blocks, near_index, near_count
):
    vmem = pl.BlockSpec(memory_space=pltpu.VMEM)
    smem = pl.BlockSpec(memory_space=pltpu.SMEM)
    hbm = pl.BlockSpec(memory_space=pl.ANY)
    dma = pltpu.SemaphoreType.DMA
    return pl.pallas_call(
        kernel,
        out_shape=pltpu.VMEM((K, W), F32),
        in_specs=[hbm, smem, hbm, hbm, hbm, hbm, hbm, hbm],
        out_specs=vmem,
        scratch_shapes=[
            pltpu.SMEM((2, SLOTS), jnp.int32),
            pltpu.SMEM((CT, RT), jnp.int32),
            pltpu.VMEM((RT, 1, B), jnp.int32),
            pltpu.VMEM((K, W), BF16),
            pltpu.VMEM((RT, CT, R, B), BF16),
            pltpu.VMEM((RT, CT, R, B), BF16),
            pltpu.VMEM((SLOTS, B, B), BF16),
            pltpu.VMEM((RT, NZ * W, B), BF16),
            pltpu.VMEM((RT, 1, B), jnp.int32),
            pltpu.VMEM((NZ, 4, K, W), BF16),
            pltpu.VMEM((RT, 4 * K, B), F32),
            pltpu.VMEM((RT, K, B), BF16),
            pltpu.VMEM((RT, CT, R, K), BF16),
            pltpu.VMEM((NX - 1, NY, K, W), BF16),
            pltpu.VMEM((NX - 1, NY, K, W), BF16),
            pltpu.VMEM((NY, K, W), F32),
            pltpu.VMEM((NY - 1, K + 16, W), jnp.int16),
            pltpu.VMEM((NY - 1, K + 16, W), jnp.int16),
            dma((7,)), dma((7,)), dma((7,)), dma((8,)), dma((8,)), dma((8,)), dma((8,)),
            dma((8,)), dma((8,)), dma((3, 4)), dma((3, 4)), dma((3,)), dma((3,)),
            pltpu.SemaphoreType.REGULAR,
        ],
        compiler_params=pltpu.CompilerParams(
            collective_id=0, has_side_effects=True, vmem_limit_bytes=60 << 20
        ),
    )(
        near_index[0, 0], near_count, tile_ranks.T, panel_order.reshape(RT, 1, B), adjoint,
        left_factor, right_factor, near_blocks[0, 0],
    )


def solution(mesh):
    placed = (
        P(None, ("row", "col")),
        P("row", None),
        P("row", "col", None, None),
        P("row", "col", None, None),
        P("row", "col"),
        P("row", "col", None, None, None),
        P("row", "col", None, None),
        P("row", "col"),
    )
    return jax.shard_map(
        local, mesh=mesh, in_specs=placed, out_specs=P(None, ("col", "row")), check_vma=False
    )
```
